256 devices in a mesh: ga: 4 (over z_hi), orb: 64 (over x, z_lo, y, core).
Axes of the slice: x: 4, y: 4, z: 8 (z_hi: 4, z_lo: 2; z = z_hi * 2 + z_lo), core: 2. Of those that a mesh axis runs over, the one named last changes fastest.
Arguments:
- coefficients: bfloat16 [2, 294912, 512], P(None, ('ga', 'orb')), may hold values from -0.01171875 to 0.01171875
- triples: int32 [3, 294912], P(None, ('ga', 'orb')), may hold values from -33 to 33
- elec_pos: float32 [3, 256], P(None, ('ga', 'orb')), may hold values from 0 to 1
- ion_pos: float32 [3, 128], replicated, may hold values from 0 to 1
- assignment: int32 [256], P(('ga', 'orb')), may hold values from 0 to 127
- rotation: int32 [256], P(('ga', 'orb')), may hold values from 0 to 63
- quad_table: float32 [64, 3, 12], replicated, may hold values from -2.4 to 2.4
- inverse_rows: float32 [256, 512], P(('ga', 'orb')), may hold values from -0.25 to 0.25
Outputs:
- ratios: float32 [256, 12], P(('ga', 'orb'))
The draws below stay inside these ranges and needn't reach their ends.
All inputs are finite; a program needn't handle non-finite values.
Results may differ from the reference program's by a relative error of at most 0.0024.
Values may be sent and summed in bfloat16 or wider, within the bound.
No kernel may reach another device: no remote copies, remote signals or barrier semaphores. Data moves between devices by JAX's collectives and lax.ppermute only.
A program may use at most 64 MiB of HBM per device.

```python
import math
import jax
import jax.numpy as jnp
from jax import lax

NORB = 512
NG = 294912
Q = 12
NION = 128
NROT = 64
NEV = 256


def touch_ends(array, rng, low, high):
    dims = array.shape
    spot = [jax.random.randint(jax.random.fold_in(rng, axis), (), 0, dims[axis]) for axis in range(len(dims))]
    array = array.at[tuple(spot)].set(low)
    longest = dims.index(max(dims))
    spot[longest] = (spot[longest] + 1) % dims[longest]
    return array.at[tuple(spot)].set(high)


def levels(key, shape, cuts, least, largest):
    gain = 1.0
    for dim, blocks in cuts:
        draws = jax.random.uniform(jax.random.fold_in(jax.random.fold_in(key, 6), dim), (blocks,), jnp.float32, least / len(cuts), largest / len(cuts))
        gain = gain * jnp.repeat(jnp.exp(draws), shape[dim] // blocks).reshape((-1,) + (1,) * (len(shape) - 1 - dim))
    return gain


def centred(rng, extent, spread, bound, split=(), held_as=jnp.bfloat16):
    level = levels(rng, extent, split, -0.22, 0.18) if split else 1.0
    result = jax.random.normal(rng, extent, jnp.float32) * spread * level
    return jnp.minimum(jnp.maximum(result, -bound), bound).astype(held_as)


def setup_inputs(seed: int = 0) -> dict:
    key_of = jax.random.split(jax.random.key(seed), 9)
    coefficients = centred(key_of[0], (2, NG, NORB), NG ** -0.5, 0.01171875, ((1, 256),))
    triples = touch_ends(jax.random.randint(key_of[1], (3, NG), -33, 34), jax.random.fold_in(key_of[1], 1), -33, 33).astype(jnp.int32)
    elec_pos = jnp.clip(1.0 * jax.random.uniform(key_of[2], (3, NEV), jnp.float32) ** levels(key_of[2], (3, NEV), ((1, 256),), -0.2, 0.2), 0.0, 1.0)
    ion_pos = jnp.clip(jax.random.uniform(key_of[3], (3, NION), jnp.float32, 0.0, 1.0), 0.0, 1.0)
    assignment = touch_ends(jax.random.randint(key_of[4], (NEV,), 0, NION), jax.random.fold_in(key_of[4], 1), 0, NION - 1).astype(jnp.int32)
    rotation = touch_ends(jax.random.randint(key_of[5], (NEV,), 0, NROT), jax.random.fold_in(key_of[5], 1), 0, NROT - 1).astype(jnp.int32)
    quad_table = centred(key_of[6], (NROT, 3, Q), 0.4, 2.4, (), jnp.float32)
    inverse_rows = centred(key_of[7], (NEV, NORB), NORB ** -0.5, 0.25, ((0, 256),), jnp.float32)
    return dict(coefficients=coefficients, triples=triples, elec_pos=elec_pos, ion_pos=ion_pos, assignment=assignment, rotation=rotation, quad_table=quad_table, inverse_rows=inverse_rows)


TWO_PI = 2.0 * math.pi

def point_coords(elec_pos, ion_pos, assignment, rotation, quad_table):
    ion_rows = jnp.take(ion_pos, assignment, axis=1)
    offsets = elec_pos - ion_rows
    radius = jnp.sqrt(lax.optimization_barrier(jnp.sum(offsets * offsets, axis=0)))
    displace = jnp.take(quad_table, rotation, axis=0)
    located = ion_rows.T[:, :, None] + radius[:, None, None] * displace
    return jnp.transpose(located, (1, 0, 2)).reshape(3, -1)

def phase_values(points, triples, coefficients):
    point_count = points.shape[1]
    wave_count = triples.shape[1]
    columns = coefficients.shape[2]
    block_rows = math.gcd(point_count, 512)
    span_cols = wave_count if wave_count <= 4096 else math.gcd(wave_count, 4096)
    waves = triples.astype(jnp.float32) * TWO_PI

    def one_block(block_points):

        def add_panel(step_index, running):
            offset = step_index * span_cols
            wave_part = lax.dynamic_slice_in_dim(waves, offset, span_cols, 1)
            angle = block_points[0][:, None] * wave_part[0][None, :] + block_points[1][:, None] * wave_part[1][None, :] + block_points[2][:, None] * wave_part[2][None, :]
            phases = jnp.concatenate([jnp.cos(angle).astype(jnp.bfloat16), jnp.sin(angle).astype(jnp.bfloat16)], axis=1)
            weights = lax.dynamic_slice_in_dim(coefficients, offset, span_cols, 1).reshape(2 * span_cols, columns)
            return running + jnp.dot(phases, weights, preferred_element_type=jnp.float32)
        initial = jnp.zeros((block_rows, columns), jnp.float32)
        return lax.fori_loop(0, wave_count // span_cols, add_panel, initial)
    blocks = jnp.transpose(points.reshape(3, point_count // block_rows, block_rows), (1, 0, 2))
    return lax.map(one_block, blocks).reshape(point_count, columns)

def reference(coefficients, triples, elec_pos, ion_pos, assignment, rotation, quad_table, inverse_rows):
    points = point_coords(elec_pos, ion_pos, assignment, rotation, quad_table)
    values = phase_values(points, triples, coefficients)
    electrons = inverse_rows.shape[0]
    shaped = values.reshape(electrons, values.shape[0] // electrons, values.shape[1])
    return lax.optimization_barrier(jnp.sum(shaped * inverse_rows[:, None, :], axis=2))
```

```python
import functools

import jax
import jax.numpy as jnp
from jax import lax
from jax.experimental import pallas as pl
from jax.experimental.pallas import tpu as pltpu
from jax.sharding import PartitionSpec as P

AXES = ("ga", "orb")
S1, S3, S5 = 6.28128008, -41.09524258, 73.58551341
A0, A1 = S1 / S5, S3 / S5
T = (0.15902982, -0.05111658, 0.02327871, -0.00620489)


def pack_kernel(rot, asg, inv, elec, ion, table, msg, scale):
    row = inv[...]
    big = jnp.max(jnp.abs(row), axis=1, keepdims=True)
    safe = jnp.maximum(big, 1e-30)
    q = jnp.round(row * (32767.0 / safe)).astype(jnp.int32)
    half = row.shape[1] // 2
    words = q[:, :half] * 65536 + q[:, half:]
    scale[...] = jnp.broadcast_to(safe * (1.0 / 32767.0), scale.shape)

    lane = lax.broadcasted_iota(jnp.int32, ion.shape, 1)
    home = jnp.sum(jnp.where(lane == asg[0], ion[...], 0.0), axis=1, keepdims=True)
    off = elec[...] - home
    radius = jnp.sqrt(jnp.sum(off * off, axis=0, keepdims=True))
    x = home + radius * table[0]
    x = x - jnp.round(x)
    y = x * 16384.0
    hi = jnp.round(y)
    lo = jnp.round((y - hi) * 32768.0)
    pw = hi.astype(jnp.int32) * 65536 + lo.astype(jnp.int32)
    flat = jnp.concatenate([pw[0:1], pw[1:2], pw[2:3]], axis=1)
    used = 3 * flat.shape[1]
    coords = jnp.concatenate(
        [flat, flat, flat, jnp.zeros((1, 128 - used), jnp.int32)], axis=1
    )
    r = lax.broadcasted_iota(jnp.int32, (24, 128), 0) % 3
    tile = jnp.where(
        r == 0,
        jnp.broadcast_to(words[:, :128], (24, 128)),
        jnp.where(
            r == 1,
            jnp.broadcast_to(words[:, 128:], (24, 128)),
            jnp.broadcast_to(coords, (24, 128)),
        ),
    )
    for i in range(msg.shape[0] // 24):
        msg[pl.ds(24 * i, 24), :] = tile


def pack(rotation, assignment, inverse_rows, elec_pos, ion_pos, quad_table, n):
    q = quad_table.shape[2]
    grid_spec = pltpu.PrefetchScalarGridSpec(
        num_scalar_prefetch=2,
        grid=(1,),
        in_specs=[
            pl.BlockSpec(inverse_rows.shape, lambda i, r, a: (0, 0)),
            pl.BlockSpec(elec_pos.shape, lambda i, r, a: (0, 0)),
            pl.BlockSpec(ion_pos.shape, lambda i, r, a: (0, 0)),
            pl.BlockSpec((1, 3, q), lambda i, r, a: (r[0], 0, 0)),
        ],
        out_specs=[
            pl.BlockSpec((3 * n, 128), lambda i, r, a: (0, 0)),
            pl.BlockSpec((1, 128), lambda i, r, a: (0, 0)),
        ],
    )
    return pl.pallas_call(
        pack_kernel,
        grid_spec=grid_spec,
        out_shape=[
            jax.ShapeDtypeStruct((3 * n, 128), jnp.int32),
            jax.ShapeDtypeStruct((1, 128), jnp.float32),
        ],
        name="pack",
    )(rotation, assignment, inverse_rows, elec_pos, ion_pos, quad_table)


def split16(word):
    low = (word << 16) >> 16
    high = (word - low) >> 16
    return high, low


def two_bf16(v):
    top = (v + 128) >> 8
    rest = v - (top << 8)
    return (top << 8).astype(jnp.float32).astype(jnp.bfloat16), rest.astype(
        jnp.float32
    ).astype(jnp.bfloat16)


NT = (((1,), (1,)), ((), ()))


def wave_kernel(msg, coef, triples, out, ih, il, pts, bt, amp, phi, u):
    n = msg.shape[0] // 3
    waves = triples.shape[1]
    q = out.shape[1]
    for i in range(2):
        high, low = split16(msg[pl.ds(i, n, stride=3), :])
        for j, v in ((i, high), (i + 2, low)):
            a, b = two_bf16(v)
            ih[:, 128 * j : 128 * j + 128] = a
            il[:, 128 * j : 128 * j + 128] = b
    high, low = split16(msg[pl.ds(2, n, stride=3), :])
    p1 = (high + 64) >> 7
    p2 = high - (p1 << 7)
    p3 = (low + 64) >> 7
    lane = lax.broadcasted_iota(jnp.int32, (n, 128), 1)
    w3 = 3 * q
    parts = jnp.where(lane < w3, p1, jnp.where(lane < 2 * w3, p2, p3))
    parts = jnp.where(lane < 3 * w3, parts, 0).astype(jnp.float32)
    which = (lane % w3) % q
    for k in range(q):
        pts[k * n : (k + 1) * n, :] = jnp.where(which == k, parts, 0.0).astype(jnp.bfloat16)
    tr = triples[...].astype(jnp.float32)
    r = lax.broadcasted_iota(jnp.int32, (128, waves), 0)
    axis = (r % w3) // q
    unit = jnp.where(r < w3, 2.0**-7, jnp.where(r < 2 * w3, 2.0**-14, 2.0**-22))
    b = jnp.where(axis == 0, tr[0:1], jnp.where(axis == 1, tr[1:2], tr[2:3])) * unit
    bt[...] = b.T.astype(jnp.bfloat16)

    step = 128

    def weigh(i, c):
        rows = pl.ds(pl.multiple_of(i * step, step), step)
        w = []
        for s in range(2):
            cs = coef[s, rows, :]
            w.append(
                lax.dot_general(cs, ih[...], NT, preferred_element_type=jnp.float32)
                + lax.dot_general(cs, il[...], NT, preferred_element_type=jnp.float32)
            )
        a, b = w
        aa, ab = jnp.abs(a), jnp.abs(b)
        big = jnp.maximum(jnp.maximum(aa, ab), 1e-30)
        t = jnp.minimum(aa, ab) / big
        t2 = t * t
        ang = ((T[3] * t2 + T[2]) * t2 + T[1]) * t2 + T[0]
        ang = ang * t
        ang = jnp.where(ab > aa, 0.25 - ang, ang)
        ang = jnp.where(a < 0.0, 0.5 - ang, ang)
        ang = jnp.where(b < 0.0, -ang, ang)
        phi[rows, :] = ang
        amp[rows, :] = big * jnp.sqrt(1.0 + t2) * (-S5)
        return c

    lax.fori_loop(0, waves // step, weigh, 0)

    for k in range(q):
        u[k] = lax.dot_general(
            bt[...], pts[k * n : (k + 1) * n, :], NT, preferred_element_type=jnp.float32
        )

    for h in range(n // 128):
        cols = slice(128 * h, 128 * h + 128)

        def tile(i, acc):
            rows = pl.ds(pl.multiple_of(i * 8, 8), 8)
            ph = phi[rows, cols]
            am = amp[rows, cols]
            new = []
            for k in range(q):
                v = u[k, rows, cols] - ph
                v = jnp.abs(v - jnp.round(v)) - 0.25
                s = v * v
                new.append(acc[k] + (((s + A1) * s + A0) * v) * am)
            return tuple(new)

        zero = jnp.zeros((8, 128), jnp.float32)
        acc = lax.fori_loop(0, waves // 8, tile, (zero,) * q, unroll=2)
        sums = [jnp.sum(a, axis=0, keepdims=True) for a in acc]
        sums.append(jnp.zeros((128 - q, 128), jnp.float32))
        out[cols, :] = jnp.concatenate(sums, axis=0).T[:, :q]


def partial_ratios(msg, coefficients, triples, n, q):
    waves = triples.shape[1]
    orbitals = coefficients.shape[2]
    vmem = pl.BlockSpec(memory_space=pltpu.VMEM)
    return pl.pallas_call(
        wave_kernel,
        out_shape=jax.ShapeDtypeStruct((n, q), jnp.float32),
        in_specs=[vmem] * 3,
        out_specs=vmem,
        scratch_shapes=[
            pltpu.VMEM((n, orbitals), jnp.bfloat16),
            pltpu.VMEM((n, orbitals), jnp.bfloat16),
            pltpu.VMEM((q * n, 128), jnp.bfloat16),
            pltpu.VMEM((waves, 128), jnp.bfloat16),
            pltpu.VMEM((waves, n), jnp.float32),
            pltpu.VMEM((waves, n), jnp.float32),
            pltpu.VMEM((q, waves, n), jnp.float32),
        ],
        compiler_params=pltpu.CompilerParams(vmem_limit_bytes=40 << 20),
        name="waves",
    )(msg, coefficients, triples)


def on_device(
    coefficients, triples, elec_pos, ion_pos, assignment, rotation, quad_table, inverse_rows, n
):
    q = quad_table.shape[2]
    msg, scale = pack(rotation, assignment, inverse_rows, elec_pos, ion_pos, quad_table, n)
    got = lax.all_to_all(msg.reshape(n, 1, 384), AXES, 0, 0, tiled=True)
    part = partial_ratios(got.reshape(3 * n, 128), coefficients, triples, n, q)
    back = lax.all_to_all(part.reshape(n, 1, q), AXES, 0, 0, tiled=True)
    return jnp.sum(back, axis=0) * scale[:, :1]


def solution(mesh):
    n = mesh.shape["ga"] * mesh.shape["orb"]
    return jax.shard_map(
        functools.partial(on_device, n=n),
        mesh=mesh,
        in_specs=(
            P(None, AXES, None),
            P(None, AXES),
            P(None, AXES),
            P(),
            P(AXES),
            P(AXES),
            P(),
            P(AXES, None),
        ),
        out_specs=P(AXES, None),
        check_vma=False,
    )
```

```python
import functools

import jax
import jax.numpy as jnp
from jax import lax
from jax.experimental import pallas as pl
from jax.experimental.pallas import tpu as pltpu
from jax.sharding import PartitionSpec as P

AXES = ("ga", "orb")
UP = 2.0**40
CHUNKS = (128, 256, 256, 256, 128, 128)
S1, S3, S5 = 6.28128008, -41.09524258, 73.58551341
A0, A1 = S1 / S5, S3 / S5
T = (0.15911832, 0.02740563, 0.00639816, 0.01881423)


def pack_kernel(rot, asg, inv, elec, ion, table, msg, scale):
    row = inv[...]
    big = jnp.max(jnp.abs(row), axis=1, keepdims=True)
    safe = jnp.maximum(big, 1e-30)
    n16 = jnp.round(row * (32767.0 / safe)).astype(jnp.int32)
    half = row.shape[1] // 2
    words = n16[:, :half] * 65536 + n16[:, half:]
    scale[...] = jnp.broadcast_to(safe * (1.0 / 32767.0 / UP), scale.shape)

    lane = lax.broadcasted_iota(jnp.int32, ion.shape, 1)
    home = jnp.sum(jnp.where(lane == asg[0], ion[...], 0.0), axis=1, keepdims=True)
    turn = lax.broadcasted_iota(jnp.int32, table.shape[1:], 1)
    total = 0.0
    homes = []
    for c in range(3):
        h = home[c : c + 1, :]
        off = elec[:, c : c + 1] - h
        homes.append(h)
        total = total + off * off
    radius = jnp.sqrt(total)
    rows = []
    for c in range(3):
        shift = jnp.sum(jnp.where(turn == rot[0], table[c], 0.0), axis=1, keepdims=True)
        x = homes[c] + radius * shift
        x = x - jnp.round(x)
        y = x * 16384.0
        hi = jnp.round(y)
        lo = jnp.round((y - hi) * 32768.0)
        rows.append(hi.astype(jnp.int32) * 65536 + lo.astype(jnp.int32))
    flat = jnp.concatenate(rows, axis=0)
    used = 3 * flat.shape[0]
    column = jnp.concatenate([flat, flat, flat, jnp.zeros((128 - used, 1), jnp.int32)], axis=0)
    square = jnp.broadcast_to(column, (128, 128)).T
    coords = square[:24]
    r = lax.broadcasted_iota(jnp.int32, (24, 128), 0) % 3
    tile = jnp.where(
        r == 0,
        jnp.broadcast_to(words[:, :128], (24, 128)),
        jnp.where(r == 1, jnp.broadcast_to(words[:, 128:], (24, 128)), coords),
    )
    for i in range(msg.shape[0] // 24):
        msg[pl.ds(24 * i, 24), :] = tile


def pack(rotation, assignment, inverse_rows, elec_pos, ion_pos, quad_table, n):
    vmem = pl.BlockSpec(memory_space=pltpu.VMEM)
    smem = pl.BlockSpec(memory_space=pltpu.SMEM)
    return pl.pallas_call(
        pack_kernel,
        in_specs=[smem, smem, vmem, vmem, vmem, vmem],
        out_specs=[vmem, vmem],
        out_shape=[
            jax.ShapeDtypeStruct((3 * n, 128), jnp.int32),
            jax.ShapeDtypeStruct((1, 128), jnp.float32),
        ],
        name="pack",
    )(
        rotation,
        assignment,
        inverse_rows,
        elec_pos.T,
        ion_pos,
        jnp.transpose(quad_table, (1, 2, 0)),
    )


def split16(word):
    low = (word << 16) >> 16
    high = (word - low) >> 16
    return high, low


def two_bf16(v):
    f = v.astype(jnp.float32) * UP
    top = f.astype(jnp.bfloat16)
    return top, (f - top.astype(jnp.float32)).astype(jnp.bfloat16)


NT = (((1,), (1,)), ((), ()))
TN = (((0,), (0,)), ((), ()))


def wave_kernel(
    own, mate, coef_hbm, triples_hbm, out, coef, triples, ih, il, parts, bt, amp, phi, ua, ub, rows_out, sem
):
    n = ih.shape[0]
    half = n // 2
    waves = triples.shape[1]
    q = out.shape[1]
    first = CHUNKS[0]
    copies = [pltpu.make_async_copy(triples_hbm, triples, sem.at[0])]
    for s in range(2):
        for lo, size in ((0, first), (first, waves - first)):
            copies.append(
                pltpu.make_async_copy(
                    coef_hbm.at[s, pl.ds(lo, size), :],
                    coef.at[s, pl.ds(lo, size), :],
                    sem.at[len(copies)],
                )
            )
    for c in (0, 1, 3, 2, 4):
        copies[c].start()
    odd = lax.axis_index("orb") % 2
    w3 = 3 * q

    def words(h, r0, i):
        at = pl.ds(i + 3 * r0, 32, stride=3)
        return jnp.where(odd == h, own[at, :], mate[at, :])

    for h in range(2):
        for r0 in range(0, half, 32):
            dst = slice(h * half + r0, h * half + r0 + 32)
            for i in range(2):
                high, low = split16(words(h, r0, i))
                for j, v in ((i, high), (i + 2, low)):
                    ih[dst, 128 * j : 128 * j + 128], il[dst, 128 * j : 128 * j + 128] = two_bf16(v)

    def weigh(lo, size):
        rows = slice(lo, lo + size)
        for s, ref in ((0, amp), (1, phi)):
            cs = coef[s, rows, :]
            ref[rows, :] = lax.dot_general(
                cs, ih[...], NT, preferred_element_type=jnp.float32
            ) + lax.dot_general(cs, il[...], NT, preferred_element_type=jnp.float32)

    copies[1].wait()
    copies[3].wait()
    weigh(0, first)

    lane = lax.broadcasted_iota(jnp.int32, (32, 128), 1)
    for h in range(2):
        for r0 in range(0, half, 32):
            high, low = split16(words(h, r0, 2))
            p1 = (high + 64) >> 7
            p2 = high - (p1 << 7)
            p3 = (low + 64) >> 7
            v = jnp.where(lane < w3, p1, jnp.where(lane < 2 * w3, p2, p3))
            parts[h * half + r0 : h * half + r0 + 32, :] = v.astype(jnp.float32).astype(jnp.bfloat16)
    which = (lane[:1] % w3) % q
    copies[0].wait()
    r = lax.broadcasted_iota(jnp.int32, (8, 128), 1)
    axis = (r % w3) // q
    unit = jnp.where(r < w3, 2.0**-7, jnp.where(r < 2 * w3, 2.0**-14, 2.0**-22))
    pick = (lax.broadcasted_iota(jnp.int32, (8, 128), 0) == axis) & (r < 3 * w3)
    spread = jnp.where(pick, unit, 0.0).astype(jnp.bfloat16)
    tr = triples[...].astype(jnp.float32)
    tr = jnp.concatenate([tr, jnp.zeros((5, waves), jnp.float32)], axis=0).T.astype(jnp.bfloat16)
    bt[...] = jnp.dot(tr, spread, preferred_element_type=jnp.float32).astype(jnp.bfloat16)

    def polar(lo, size):
        for g in range(lo, lo + size, 16):
            rows = slice(g, g + 16)
            a, b = amp[rows, :], phi[rows, :]
            aa, ab = jnp.abs(a), jnp.abs(b)
            h = jnp.maximum(a * a + b * b, 1e-36)
            r = lax.rsqrt(h)
            amp[rows, :] = h * r * (-S5)
            t = jnp.minimum(aa, ab) * r
            t2 = t * t
            ang = ((T[3] * t2 + T[2]) * t2 + T[1]) * t2 + T[0]
            ang = ang * t
            ang = jnp.where(ab > aa, 0.25 - ang, ang)
            ang = jnp.where(a < 0.0, 0.5 - ang, ang)
            phi[rows, :] = jnp.where(b < 0.0, -ang, ang)

    def angles(k, ref):
        mask = jnp.where(which == k, 1.0, 0.0).astype(jnp.bfloat16)
        ref[...] = lax.dot_general(
            bt[...], parts[...] * mask, NT, preferred_element_type=jnp.float32
        )

    def contract(k, ref):
        acc = jnp.zeros((8, n), jnp.float32)
        for g in range(0, waves, 8):
            rows = slice(g, g + 8)
            v = ref[rows, :] - phi[rows, :]
            v = jnp.abs(v - jnp.round(v)) - 0.25
            s = v * v
            acc = acc + (((s + A1) * s + A0) * v) * amp[rows, :]
        rows_out[pl.ds(k, 1), :] = jnp.sum(acc, axis=0, keepdims=True)

    copies[2].wait()
    copies[4].wait()
    lo = 0
    for size, ahead in zip(CHUNKS, CHUNKS[1:]):
        weigh(lo + size, ahead)
        polar(lo, size)
        lo += size
    angles(0, ua)
    polar(lo, CHUNKS[-1])

    def pair(j, c):
        angles(2 * j + 1, ub)
        contract(2 * j, ua)
        angles(jnp.minimum(2 * j + 2, q - 1), ua)
        contract(2 * j + 1, ub)
        return c

    lax.fori_loop(0, q // 2, pair, 0)
    for h in range(2):
        turned = rows_out[:, h * half : h * half + half].T
        out[pl.ds(h, half, stride=2), :] = turned[:, :q]


def partial_ratios(own, mate, coefficients, triples, n, q):
    waves = triples.shape[1]
    orbitals = coefficients.shape[2]
    vmem = pl.BlockSpec(memory_space=pltpu.VMEM)
    hbm = pl.BlockSpec(memory_space=pltpu.HBM)
    return pl.pallas_call(
        wave_kernel,
        out_shape=jax.ShapeDtypeStruct((n, q), jnp.float32),
        in_specs=[vmem, vmem, hbm, hbm],
        out_specs=vmem,
        scratch_shapes=[
            pltpu.VMEM(coefficients.shape, jnp.bfloat16),
            pltpu.VMEM(triples.shape, jnp.int32),
            pltpu.VMEM((n, orbitals), jnp.bfloat16),
            pltpu.VMEM((n, orbitals), jnp.bfloat16),
            pltpu.VMEM((n, 128), jnp.bfloat16),
            pltpu.VMEM((waves, 128), jnp.bfloat16),
            pltpu.VMEM((waves, n), jnp.float32),
            pltpu.VMEM((waves, n), jnp.float32),
            pltpu.VMEM((waves, n), jnp.float32),
            pltpu.VMEM((waves, n), jnp.float32),
            pltpu.VMEM((128, n), jnp.float32),
            pltpu.SemaphoreType.DMA((5,)),
        ],
        compiler_params=pltpu.CompilerParams(vmem_limit_bytes=52 << 20),
        name="waves",
    )(own, mate, coefficients, triples)


def on_device(
    coefficients, triples, elec_pos, ion_pos, assignment, rotation, quad_table, inverse_rows, n
):
    q = quad_table.shape[2]
    half = n // 2
    msg, scale = pack(rotation, assignment, inverse_rows, elec_pos, ion_pos, quad_table, half)
    sides = [list(range(c, n, 2)) for c in range(2)]
    own = lax.all_to_all(
        msg.reshape(half, 1, 384), AXES, 0, 0, axis_index_groups=sides, tiled=True
    ).reshape(3 * half, 128)
    mate = lax.ppermute(own, AXES, [(i, i ^ 1) for i in range(n)])
    part = partial_ratios(own, mate, coefficients, triples, n, q)
    back = lax.all_to_all(part.reshape(n, 1, q), AXES, 0, 0, tiled=True)
    return jnp.sum(back * scale[0, 0], axis=0)


def solution(mesh):
    n = mesh.shape["ga"] * mesh.shape["orb"]
    return jax.shard_map(
        functools.partial(on_device, n=n),
        mesh=mesh,
        in_specs=(
            P(None, AXES, None),
            P(None, AXES),
            P(None, AXES),
            P(),
            P(AXES),
            P(AXES),
            P(),
            P(AXES, None),
        ),
        out_specs=P(AXES, None),
        check_vma=False,
    )
```

```python
import functools

import jax
import jax.numpy as jnp
from jax import lax
from jax.experimental import pallas as pl
from jax.experimental.pallas import tpu as pltpu
from jax.sharding import PartitionSpec as P

AXES = ("ga", "orb")
UP = 2.0**40
KEPT_ROWS = 640
CHUNKS = (128, 256, 256, 256, 128, 128)
C0, C1, C2 = 0.26392367, -1.2978812, 28.72800057
MEAN = 0.0348596450351644
T = (0.15911832, 0.02740563, 0.00639816, 0.01881423)


def pack_kernel(rot, asg, inv, elec, ion, table, triples, msg, kept, eight, sem):
    eight[...] = jnp.zeros_like(eight)
    eight[0:3, :] = triples[...]
    keep = pltpu.make_async_copy(eight, kept.at[pl.ds(0, 8), :], sem)
    keep.start()
    row = inv[...]
    big = jnp.max(jnp.abs(row), axis=1, keepdims=True)
    safe = jnp.maximum(big, 1e-30)
    power = jnp.floor(jnp.log2(32767.0 / safe))
    n16 = jnp.clip(jnp.round(row * jnp.exp2(power)), -32767.0, 32767.0).astype(jnp.int32)
    half = row.shape[1] // 2
    words = n16[:, :half] * 65536 + n16[:, half:]

    lane = lax.broadcasted_iota(jnp.int32, ion.shape, 1)
    home = jnp.sum(jnp.where(lane == asg[0], ion[...], 0.0), axis=1, keepdims=True)
    turn = lax.broadcasted_iota(jnp.int32, table.shape[1:], 1)
    total = 0.0
    homes = []
    for c in range(3):
        h = home[c : c + 1, :]
        off = elec[:, c : c + 1] - h
        homes.append(h)
        total = total + off * off
    radius = jnp.sqrt(total)
    rows = []
    for c in range(3):
        shift = jnp.sum(jnp.where(turn == rot[0], table[c], 0.0), axis=1, keepdims=True)
        x = homes[c] + radius * shift
        x = x - jnp.round(x)
        y = x * 16384.0
        hi = jnp.round(y)
        lo = jnp.round((y - hi) * 32768.0)
        rows.append(hi.astype(jnp.int32) * 65536 + lo.astype(jnp.int32))
    flat = jnp.concatenate(rows, axis=0)
    used = 3 * flat.shape[0]
    column = jnp.concatenate(
        [flat, flat, flat, jnp.zeros((127 - used, 1), jnp.int32), power.astype(jnp.int32)], axis=0
    )
    square = jnp.broadcast_to(column, (128, 128)).T
    coords = square[:24]
    r = lax.broadcasted_iota(jnp.int32, (24, 128), 0) % 3
    tile = jnp.where(
        r == 0,
        jnp.broadcast_to(words[:, :128], (24, 128)),
        jnp.where(r == 1, jnp.broadcast_to(words[:, 128:], (24, 128)), coords),
    )
    for i in range(msg.shape[0] // 24):
        msg[pl.ds(24 * i, 24), :] = tile
    keep.wait()


def pack(rotation, assignment, inverse_rows, elec_pos, ion_pos, quad_table, triples, n):
    vmem = pl.BlockSpec(memory_space=pltpu.VMEM)
    smem = pl.BlockSpec(memory_space=pltpu.SMEM)
    return pl.pallas_call(
        pack_kernel,
        in_specs=[smem, smem, vmem, vmem, vmem, vmem, vmem],
        out_specs=[vmem, pl.BlockSpec(memory_space=pltpu.HBM)],
        out_shape=[
            jax.ShapeDtypeStruct((3 * n, 128), jnp.int32),
            jax.ShapeDtypeStruct((KEPT_ROWS, triples.shape[1]), jnp.int32),
        ],
        scratch_shapes=[
            pltpu.VMEM((8, triples.shape[1]), jnp.int32),
            pltpu.SemaphoreType.DMA,
        ],
        name="pack",
    )(
        rotation,
        assignment,
        inverse_rows,
        elec_pos.T,
        ion_pos,
        jnp.transpose(quad_table, (1, 2, 0)),
        triples,
    )


def split16(word):
    low = (word << 16) >> 16
    high = (word - low) >> 16
    return high, low


def two_bf16(v):
    f = v.astype(jnp.float32) * UP
    top = f.astype(jnp.bfloat16)
    return top, (f - top.astype(jnp.float32)).astype(jnp.bfloat16)


NT = (((1,), (1,)), ((), ()))
TN = (((0,), (0,)), ((), ()))


def wave_kernel(
    own, mate, coef_hbm, triples_hbm, out, coef, triples, ih, il, parts, bt, amp, phi, ua, ub, rows_out, base, unit_of, sem
):
    n = ih.shape[0]
    half = n // 2
    waves = triples.shape[1]
    q = out.shape[1]
    first = CHUNKS[0]
    copies = [pltpu.make_async_copy(triples_hbm.at[pl.ds(0, 8), :], triples, sem.at[0])]
    for s in range(2):
        for lo, size in ((0, first), (first, waves - first)):
            copies.append(
                pltpu.make_async_copy(
                    coef_hbm.at[s, pl.ds(lo, size), :],
                    coef.at[s, pl.ds(lo, size), :],
                    sem.at[len(copies)],
                )
            )
    for c in (0, 1, 3, 2, 4):
        copies[c].start()
    odd = lax.axis_index("orb") % 2
    w3 = 3 * q

    def words(h, r0, i):
        at = pl.ds(i + 3 * r0, 32, stride=3)
        return jnp.where(odd == h, own[at, :], mate[at, :])

    for h in range(2):
        for r0 in range(0, half, 32):
            dst = slice(h * half + r0, h * half + r0 + 32)
            for i in range(2):
                high, low = split16(words(h, r0, i))
                for j, v in ((i, high), (i + 2, low)):
                    ih[dst, 128 * j : 128 * j + 128], il[dst, 128 * j : 128 * j + 128] = two_bf16(v)

    def weigh(lo, size):
        rows = slice(lo, lo + size)
        for s, ref in ((0, amp), (1, phi)):
            cs = coef[s, rows, :]
            ref[rows, :] = lax.dot_general(
                cs, ih[...], NT, preferred_element_type=jnp.float32
            ) + lax.dot_general(cs, il[...], NT, preferred_element_type=jnp.float32)

    copies[1].wait()
    copies[3].wait()
    weigh(0, first)

    lane = lax.broadcasted_iota(jnp.int32, (32, 128), 1)
    for h in range(2):
        for r0 in range(0, half, 32):
            word = words(h, r0, 2)
            scale = jnp.exp2(-word[:, 127:].astype(jnp.float32)) * (1.0 / UP)
            unit_of[h * half + r0 : h * half + r0 + 32, :] = jnp.broadcast_to(scale, (32, 128))
            high, low = split16(word)
            p1 = (high + 64) >> 7
            p2 = high - (p1 << 7)
            p3 = (low + 64) >> 7
            v = jnp.where(lane < w3, p1, jnp.where(lane < 2 * w3, p2, p3))
            parts[h * half + r0 : h * half + r0 + 32, :] = v.astype(jnp.float32).astype(jnp.bfloat16)
    which = (lane[:1] % w3) % q
    copies[0].wait()
    r = lax.broadcasted_iota(jnp.int32, (8, 128), 1)
    axis = (r % w3) // q
    unit = jnp.where(r < w3, 2.0**-7, jnp.where(r < 2 * w3, 2.0**-14, 2.0**-22))
    pick = (lax.broadcasted_iota(jnp.int32, (8, 128), 0) == axis) & (r < 3 * w3)
    spread = jnp.where(pick, unit, 0.0).astype(jnp.bfloat16)
    tr = triples[...].astype(jnp.float32).T.astype(jnp.bfloat16)
    bt[...] = jnp.dot(tr, spread, preferred_element_type=jnp.float32).astype(jnp.bfloat16)

    def polar(lo, count):
        total = base[...]
        for g in range(lo, lo + count, 16):
            rows = slice(g, g + 16)
            a, b = amp[rows, :], phi[rows, :]
            aa, ab = jnp.abs(a), jnp.abs(b)
            h = jnp.maximum(a * a + b * b, 1e-36)
            r = lax.rsqrt(h)
            size = h * r * C2
            amp[rows, :] = size
            total = total + size[:8] + size[8:]
            t = jnp.minimum(aa, ab) * r
            t2 = t * t
            ang = ((T[3] * t2 + T[2]) * t2 + T[1]) * t2 + T[0]
            ang = ang * t
            ang = jnp.where(ab > aa, 0.25 - ang, ang)
            ang = jnp.where(a < 0.0, 0.5 - ang, ang)
            phi[rows, :] = jnp.where(b < 0.0, -ang, ang)
        base[...] = total

    def angles(k, ref):
        mask = jnp.where(which == k, 1.0, 0.0).astype(jnp.bfloat16)
        ref[...] = lax.dot_general(
            bt[...], parts[...] * mask, NT, preferred_element_type=jnp.float32
        )

    def contract(k, ref):
        acc = jnp.zeros((8, n), jnp.float32)
        for g in range(0, waves, 8):
            rows = slice(g, g + 8)
            v = ref[rows, :] - phi[rows, :]
            v = v - jnp.round(v)
            s = v * v
            w = (s + C1) * s + C0
            acc = acc + (w * w) * amp[rows, :]
        rows_out[pl.ds(k, 1), :] = jnp.sum(acc - base[...], axis=0, keepdims=True)

    copies[2].wait()
    copies[4].wait()
    base[...] = jnp.zeros_like(base)
    lo = 0
    for size, ahead in zip(CHUNKS, CHUNKS[1:]):
        weigh(lo + size, ahead)
        polar(lo, size)
        lo += size
    angles(0, ua)
    polar(lo, CHUNKS[-1])
    base[...] = base[...] * MEAN

    def pair(j, c):
        angles(2 * j + 1, ub)
        contract(2 * j, ua)
        angles(jnp.minimum(2 * j + 2, q - 1), ua)
        contract(2 * j + 1, ub)
        return c

    lax.fori_loop(0, q // 2, pair, 0)
    for h in range(2):
        turned = rows_out[:, h * half : h * half + half].T
        out[pl.ds(h, half, stride=2), :] = (turned * unit_of[h * half : h * half + half, :])[:, :q]


def partial_ratios(own, mate, coefficients, triples, n, q):
    waves = triples.shape[1]
    orbitals = coefficients.shape[2]
    vmem = pl.BlockSpec(memory_space=pltpu.VMEM)
    hbm = pl.BlockSpec(memory_space=pltpu.HBM)
    return pl.pallas_call(
        wave_kernel,
        out_shape=jax.ShapeDtypeStruct((n, q), jnp.float32),
        in_specs=[vmem, vmem, hbm, hbm],
        out_specs=vmem,
        scratch_shapes=[
            pltpu.VMEM(coefficients.shape, jnp.bfloat16),
            pltpu.VMEM((8, waves), jnp.int32),
            pltpu.VMEM((n, orbitals), jnp.bfloat16),
            pltpu.VMEM((n, orbitals), jnp.bfloat16),
            pltpu.VMEM((n, 128), jnp.bfloat16),
            pltpu.VMEM((waves, 128), jnp.bfloat16),
            pltpu.VMEM((waves, n), jnp.float32),
            pltpu.VMEM((waves, n), jnp.float32),
            pltpu.VMEM((waves, n), jnp.float32),
            pltpu.VMEM((waves, n), jnp.float32),
            pltpu.VMEM((128, n), jnp.float32),
            pltpu.VMEM((8, n), jnp.float32),
            pltpu.VMEM((n, 128), jnp.float32),
            pltpu.SemaphoreType.DMA((5,)),
        ],
        compiler_params=pltpu.CompilerParams(vmem_limit_bytes=52 << 20),
        name="waves",
    )(own, mate, coefficients, triples)


def on_device(
    coefficients, triples, elec_pos, ion_pos, assignment, rotation, quad_table, inverse_rows, n
):
    q = quad_table.shape[2]
    half = n // 2
    msg, kept = pack(
        rotation, assignment, inverse_rows, elec_pos, ion_pos, quad_table, triples, half
    )
    sides = [list(range(c, n, 2)) for c in range(2)]
    own = lax.all_to_all(
        msg.reshape(half, 1, 384), AXES, 0, 0, axis_index_groups=sides, tiled=True
    ).reshape(3 * half, 128)
    mate = lax.ppermute(own, AXES, [(i, i ^ 1) for i in range(n)])
    part = partial_ratios(own, mate, coefficients, kept, n, q)
    back = lax.all_to_all(part.reshape(n, 1, q), AXES, 0, 0, tiled=True)
    return jnp.sum(back, axis=0)


def solution(mesh):
    n = mesh.shape["ga"] * mesh.shape["orb"]
    return jax.shard_map(
        functools.partial(on_device, n=n),
        mesh=mesh,
        in_specs=(
            P(None, AXES, None),
            P(None, AXES),
            P(None, AXES),
            P(),
            P(AXES),
            P(AXES),
            P(),
            P(AXES, None),
        ),
        out_specs=P(AXES, None),
        check_vma=False,
    )
```

```python
import functools

import jax
import jax.numpy as jnp
from jax import lax
from jax.experimental import pallas as pl
from jax.experimental.pallas import tpu as pltpu
from jax.sharding import PartitionSpec as P

AXES = ("ga", "orb")
UP = 2.0**40
KEPT_ROWS = 640
CHUNKS = (128, 256, 256, 256, 128, 128)
C0, C1, C2 = 0.26392367, -1.2978812, 28.72800057
MEAN = 0.0348596450351644
T = tuple(
    t * 2.0 ** (0.5 - i) for i, t in enumerate((0.15911832, 0.02740563, 0.00639816, 0.01881423))
)


def pack_kernel(rot, asg, inv, elec, ion, table, triples, msg, kept, eight, sem):
    eight[...] = jnp.zeros_like(eight)
    eight[0:3, :] = triples[...]
    keep = pltpu.make_async_copy(eight, kept.at[pl.ds(0, 8), :], sem)
    keep.start()
    row = inv[...]
    big = jnp.max(jnp.abs(row), axis=1, keepdims=True)
    safe = jnp.maximum(big, 1e-30)
    power = jnp.floor(jnp.log2(32767.0 / safe))
    n16 = jnp.clip(jnp.round(row * jnp.exp2(power)), -32767.0, 32767.0).astype(jnp.int32)
    half = row.shape[1] // 2
    words = n16[:, :half] * 65536 + n16[:, half:]

    lane = lax.broadcasted_iota(jnp.int32, ion.shape, 1)
    home = jnp.sum(jnp.where(lane == asg[0], ion[...], 0.0), axis=1, keepdims=True)
    turn = lax.broadcasted_iota(jnp.int32, table.shape[1:], 1)
    total = 0.0
    homes = []
    for c in range(3):
        h = home[c : c + 1, :]
        off = elec[:, c : c + 1] - h
        homes.append(h)
        total = total + off * off
    radius = jnp.sqrt(total)
    rows = []
    for c in range(3):
        shift = jnp.sum(jnp.where(turn == rot[0], table[c], 0.0), axis=1, keepdims=True)
        x = homes[c] + radius * shift
        x = x - jnp.round(x)
        y = x * 16384.0
        hi = jnp.round(y)
        lo = jnp.round((y - hi) * 32768.0)
        rows.append(hi.astype(jnp.int32) * 65536 + lo.astype(jnp.int32))
    flat = jnp.concatenate(rows, axis=0)
    used = 3 * flat.shape[0]
    column = jnp.concatenate(
        [flat, flat, flat, jnp.zeros((127 - used, 1), jnp.int32), power.astype(jnp.int32)], axis=0
    )
    square = jnp.broadcast_to(column, (128, 128)).T
    coords = square[:24]
    r = lax.broadcasted_iota(jnp.int32, (24, 128), 0) % 3
    tile = jnp.where(
        r == 0,
        jnp.broadcast_to(words[:, :128], (24, 128)),
        jnp.where(r == 1, jnp.broadcast_to(words[:, 128:], (24, 128)), coords),
    )
    for i in range(msg.shape[0] // 24):
        msg[pl.ds(24 * i, 24), :] = tile
    keep.wait()


def pack(rotation, assignment, inverse_rows, elec_pos, ion_pos, quad_table, triples, n):
    vmem = pl.BlockSpec(memory_space=pltpu.VMEM)
    smem = pl.BlockSpec(memory_space=pltpu.SMEM)
    return pl.pallas_call(
        pack_kernel,
        in_specs=[smem, smem, vmem, vmem, vmem, vmem, vmem],
        out_specs=[vmem, pl.BlockSpec(memory_space=pltpu.HBM)],
        out_shape=[
            jax.ShapeDtypeStruct((3 * n, 128), jnp.int32),
            jax.ShapeDtypeStruct((KEPT_ROWS, triples.shape[1]), jnp.int32),
        ],
        scratch_shapes=[
            pltpu.VMEM((8, triples.shape[1]), jnp.int32),
            pltpu.SemaphoreType.DMA,
        ],
        name="pack",
    )(
        rotation,
        assignment,
        inverse_rows,
        elec_pos.T,
        ion_pos,
        jnp.transpose(quad_table, (1, 2, 0)),
        triples,
    )


def split16(word):
    low = (word << 16) >> 16
    high = (word - low) >> 16
    return high, low


def two_bf16(v):
    f = v.astype(jnp.float32) * UP
    top = f.astype(jnp.bfloat16)
    return top, (f - top.astype(jnp.float32)).astype(jnp.bfloat16)


NT = (((1,), (1,)), ((), ()))
TN = (((0,), (0,)), ((), ()))


def wave_kernel(
    own, mate, coef_hbm, triples_hbm, out, coef, triples, ih, il, parts, bt, amp, phi, ua, ub, rows_out, base, unit_of, sem
):
    n = ih.shape[0]
    half = n // 2
    waves = triples.shape[1]
    q = out.shape[1]
    first = CHUNKS[0]
    copies = [pltpu.make_async_copy(triples_hbm.at[pl.ds(0, 8), :], triples, sem.at[0])]
    for s in range(2):
        for lo, size in ((0, first), (first, waves - first)):
            copies.append(
                pltpu.make_async_copy(
                    coef_hbm.at[s, pl.ds(lo, size), :],
                    coef.at[s, pl.ds(lo, size), :],
                    sem.at[len(copies)],
                )
            )
    for c in (0, 1, 3, 2, 4):
        copies[c].start()
    odd = lax.axis_index("orb") % 2
    w3 = 3 * q

    def words(h, r0, i):
        at = pl.ds(i + 3 * r0, 32, stride=3)
        return jnp.where(odd == h, own[at, :], mate[at, :])

    for h in range(2):
        for r0 in range(0, half, 32):
            dst = slice(h * half + r0, h * half + r0 + 32)
            for i in range(2):
                high, low = split16(words(h, r0, i))
                for j, v in ((i, high), (i + 2, low)):
                    ih[dst, 128 * j : 128 * j + 128], il[dst, 128 * j : 128 * j + 128] = two_bf16(v)

    def weigh(lo, size):
        rows = slice(lo, lo + size)
        for s, ref in ((0, amp), (1, phi)):
            cs = coef[s, rows, :]
            ref[rows, :] = lax.dot_general(
                cs, ih[...], NT, preferred_element_type=jnp.float32
            ) + lax.dot_general(cs, il[...], NT, preferred_element_type=jnp.float32)

    copies[0].wait()
    copies[1].wait()
    copies[3].wait()
    weigh(0, first)

    lane = lax.broadcasted_iota(jnp.int32, (32, 128), 1)
    for h in range(2):
        for r0 in range(0, half, 32):
            word = words(h, r0, 2)
            scale = jnp.exp2(-word[:, 127:].astype(jnp.float32)) * (C2 / UP)
            unit_of[h * half + r0 : h * half + r0 + 32, :] = jnp.broadcast_to(scale, (32, 128))
            high, low = split16(word)
            p1 = (high + 64) >> 7
            p2 = high - (p1 << 7)
            p3 = (low + 64) >> 7
            v = jnp.where(lane < w3, p1, jnp.where(lane < 2 * w3, p2, p3))
            parts[h * half + r0 : h * half + r0 + 32, :] = v.astype(jnp.float32).astype(jnp.bfloat16)
    which = (lane[:1] % w3) % q
    r = lax.broadcasted_iota(jnp.int32, (8, 128), 1)
    axis = (r % w3) // q
    unit = jnp.where(r < w3, 2.0**-7, jnp.where(r < 2 * w3, 2.0**-14, 2.0**-22))
    pick = (lax.broadcasted_iota(jnp.int32, (8, 128), 0) == axis) & (r < 3 * w3)
    spread = jnp.where(pick, unit, 0.0).astype(jnp.bfloat16)
    tr = triples[...].astype(jnp.float32).T.astype(jnp.bfloat16)
    bt[...] = jnp.dot(tr, spread, preferred_element_type=jnp.float32).astype(jnp.bfloat16)

    def polar(lo, count):
        total = base[...]
        for g in range(lo, lo + count, 16):
            rows = slice(g, g + 16)
            a, b = amp[rows, :], phi[rows, :]
            h = jnp.maximum(a * a + b * b, 1e-36)
            r = lax.rsqrt(h)
            size = h * r
            x = (b * r) * lax.rsqrt(1.0 + jnp.abs(a) * r)
            x2 = x * x
            ang = (((T[3] * x2 + T[2]) * x2 + T[1]) * x2 + T[0]) * x
            amp[rows, :] = size
            phi[rows, :] = jnp.where(a < 0.0, 0.5 - ang, ang)
            total = total + size[:8] + size[8:]
        base[...] = total

    def angles(k, ref):
        mask = jnp.where(which == k, 1.0, 0.0).astype(jnp.bfloat16)
        ref[...] = lax.dot_general(
            bt[...], parts[...] * mask, NT, preferred_element_type=jnp.float32
        )

    def contract(k, ref):
        acc = jnp.zeros((8, n), jnp.float32)
        for g in range(0, waves, 8):
            rows = slice(g, g + 8)
            v = ref[rows, :] - phi[rows, :]
            v = v - jnp.round(v)
            s = v * v
            w = (s + C1) * s + C0
            acc = acc + (w * w) * amp[rows, :]
        rows_out[pl.ds(k, 1), :] = jnp.sum(acc - base[...], axis=0, keepdims=True)

    copies[2].wait()
    copies[4].wait()
    base[...] = jnp.zeros_like(base)
    lo = 0
    for i, (size, ahead) in enumerate(zip(CHUNKS, CHUNKS[1:])):
        weigh(lo + size, ahead)
        if i == 2:
            angles(0, ua)
        polar(lo, size)
        lo += size
    polar(lo, CHUNKS[-1])
    base[...] = base[...] * MEAN

    for k in range(q):
        held, free = (ua, ub) if k % 2 == 0 else (ub, ua)
        if k + 1 < q:
            angles(k + 1, free)
        contract(k, held)
    for h in range(2):
        turned = rows_out[:, h * half : h * half + half].T
        out[pl.ds(h, half, stride=2), :] = (turned * unit_of[h * half : h * half + half, :])[:, :q]


def partial_ratios(own, mate, coefficients, triples, n, q):
    waves = triples.shape[1]
    orbitals = coefficients.shape[2]
    vmem = pl.BlockSpec(memory_space=pltpu.VMEM)
    hbm = pl.BlockSpec(memory_space=pltpu.HBM)
    return pl.pallas_call(
        wave_kernel,
        out_shape=jax.ShapeDtypeStruct((n, q), jnp.float32),
        in_specs=[vmem, vmem, hbm, hbm],
        out_specs=vmem,
        scratch_shapes=[
            pltpu.VMEM(coefficients.shape, jnp.bfloat16),
            pltpu.VMEM((8, waves), jnp.int32),
            pltpu.VMEM((n, orbitals), jnp.bfloat16),
            pltpu.VMEM((n, orbitals), jnp.bfloat16),
            pltpu.VMEM((n, 128), jnp.bfloat16),
            pltpu.VMEM((waves, 128), jnp.bfloat16),
            pltpu.VMEM((waves, n), jnp.float32),
            pltpu.VMEM((waves, n), jnp.float32),
            pltpu.VMEM((waves, n), jnp.float32),
            pltpu.VMEM((waves, n), jnp.float32),
            pltpu.VMEM((128, n), jnp.float32),
            pltpu.VMEM((8, n), jnp.float32),
            pltpu.VMEM((n, 128), jnp.float32),
            pltpu.SemaphoreType.DMA((5,)),
        ],
        compiler_params=pltpu.CompilerParams(vmem_limit_bytes=52 << 20),
        name="waves",
    )(own, mate, coefficients, triples)


def on_device(
    coefficients, triples, elec_pos, ion_pos, assignment, rotation, quad_table, inverse_rows, n
):
    q = quad_table.shape[2]
    half = n // 2
    msg, kept = pack(
        rotation, assignment, inverse_rows, elec_pos, ion_pos, quad_table, triples, half
    )
    sides = [list(range(c, n, 2)) for c in range(2)]
    own = lax.all_to_all(
        msg.reshape(half, 1, 384), AXES, 0, 0, axis_index_groups=sides, tiled=True
    ).reshape(3 * half, 128)
    mate = lax.ppermute(own, AXES, [(i, i ^ 1) for i in range(n)])
    part = partial_ratios(own, mate, coefficients, kept, n, q)
    back = lax.all_to_all(part.reshape(n, 1, q), AXES, 0, 0, tiled=True)
    return jnp.sum(back, axis=0)


def solution(mesh):
    n = mesh.shape["ga"] * mesh.shape["orb"]
    return jax.shard_map(
        functools.partial(on_device, n=n),
        mesh=mesh,
        in_specs=(
            P(None, AXES, None),
            P(None, AXES),
            P(None, AXES),
            P(),
            P(AXES),
            P(AXES),
            P(),
            P(AXES, None),
        ),
        out_specs=P(AXES, None),
        check_vma=False,
    )
```

```python
import functools

import jax
import jax.numpy as jnp
from jax import lax
from jax.experimental import pallas as pl
from jax.experimental.pallas import tpu as pltpu
from jax.sharding import PartitionSpec as P

AXES = ("ga", "orb")
UP = 2.0**40
KEPT_ROWS = 640
CHUNKS = (128, 256, 256, 256, 256)
C0, C1, C2 = 0.26392367, -1.2978812, 28.72800057
MEAN = 0.0348596450351644
T = tuple(
    t * 2.0 ** (0.5 - i) for i, t in enumerate((0.15911832, 0.02740563, 0.00639816, 0.01881423))
)


def pack_kernel(rot, asg, inv, elec, ion, table, triples, msg, kept, eight, sem):
    eight[...] = jnp.zeros_like(eight)
    eight[0:3, :] = triples[...]
    keep = pltpu.make_async_copy(eight, kept.at[pl.ds(0, 8), :], sem)
    keep.start()
    row = inv[...]
    big = jnp.max(jnp.abs(row), axis=1, keepdims=True)
    safe = jnp.maximum(big, 1e-30)
    power = jnp.floor(jnp.log2(32767.0 / safe))
    n16 = jnp.clip(jnp.round(row * jnp.exp2(power)), -32767.0, 32767.0).astype(jnp.int32)
    half = row.shape[1] // 2
    words = n16[:, :half] * 65536 + n16[:, half:]

    lane = lax.broadcasted_iota(jnp.int32, ion.shape, 1)
    home = jnp.sum(jnp.where(lane == asg[0], ion[...], 0.0), axis=1, keepdims=True)
    turn = lax.broadcasted_iota(jnp.int32, table.shape[1:], 1)
    total = 0.0
    homes = []
    for c in range(3):
        h = home[c : c + 1, :]
        off = elec[:, c : c + 1] - h
        homes.append(h)
        total = total + off * off
    radius = jnp.sqrt(total)
    rows = []
    for c in range(3):
        shift = jnp.sum(jnp.where(turn == rot[0], table[c], 0.0), axis=1, keepdims=True)
        x = homes[c] + radius * shift
        x = x - jnp.round(x)
        y = x * 16384.0
        hi = jnp.round(y)
        lo = jnp.round((y - hi) * 32768.0)
        rows.append(hi.astype(jnp.int32) * 65536 + lo.astype(jnp.int32))
    flat = jnp.concatenate(rows, axis=0)
    used = 3 * flat.shape[0]
    column = jnp.concatenate(
        [flat, flat, flat, jnp.zeros((127 - used, 1), jnp.int32), power.astype(jnp.int32)], axis=0
    )
    square = jnp.broadcast_to(column, (128, 128)).T
    coords = square[:24]
    r = lax.broadcasted_iota(jnp.int32, (24, 128), 0) % 3
    tile = jnp.where(
        r == 0,
        jnp.broadcast_to(words[:, :128], (24, 128)),
        jnp.where(r == 1, jnp.broadcast_to(words[:, 128:], (24, 128)), coords),
    )
    for i in range(msg.shape[0] // 24):
        msg[pl.ds(24 * i, 24), :] = tile
    keep.wait()


def pack(rotation, assignment, inverse_rows, elec_pos, ion_pos, quad_table, triples, n):
    vmem = pl.BlockSpec(memory_space=pltpu.VMEM)
    smem = pl.BlockSpec(memory_space=pltpu.SMEM)
    return pl.pallas_call(
        pack_kernel,
        in_specs=[smem, smem, vmem, vmem, vmem, vmem, vmem],
        out_specs=[vmem, pl.BlockSpec(memory_space=pltpu.HBM)],
        out_shape=[
            jax.ShapeDtypeStruct((3 * n, 128), jnp.int32),
            jax.ShapeDtypeStruct((KEPT_ROWS, triples.shape[1]), jnp.int32),
        ],
        scratch_shapes=[
            pltpu.VMEM((8, triples.shape[1]), jnp.int32),
            pltpu.SemaphoreType.DMA,
        ],
        name="pack",
    )(
        rotation,
        assignment,
        inverse_rows,
        elec_pos.T,
        ion_pos,
        jnp.transpose(quad_table, (1, 2, 0)),
        triples,
    )


def split16(word):
    low = (word << 16) >> 16
    high = (word - low) >> 16
    return high, low


def two_bf16(v):
    f = v.astype(jnp.float32) * UP
    top = f.astype(jnp.bfloat16)
    return top, (f - top.astype(jnp.float32)).astype(jnp.bfloat16)


NT = (((1,), (1,)), ((), ()))
TN = (((0,), (0,)), ((), ()))


def wave_kernel(
    own, mate, coef_hbm, triples_hbm, out, coef, triples, ih, il, parts, bt, amp, phi, ua, ub, rows_out, base, unit_of, sem
):
    n = ih.shape[0]
    half = n // 2
    waves = triples.shape[1]
    q = out.shape[1]
    first = CHUNKS[0]
    copies = [pltpu.make_async_copy(triples_hbm.at[pl.ds(0, 8), :], triples, sem.at[0])]
    for s in range(2):
        for lo, size in ((0, first), (first, waves - first)):
            copies.append(
                pltpu.make_async_copy(
                    coef_hbm.at[s, pl.ds(lo, size), :],
                    coef.at[s, pl.ds(lo, size), :],
                    sem.at[len(copies)],
                )
            )
    for c in (0, 1, 3, 2, 4):
        copies[c].start()
    odd = lax.axis_index("orb") % 2
    w3 = 3 * q

    def words(h, r0, i):
        at = pl.ds(i + 3 * r0, 32, stride=3)
        return jnp.where(odd == h, own[at, :], mate[at, :])

    for h in range(2):
        for r0 in range(0, half, 32):
            dst = slice(h * half + r0, h * half + r0 + 32)
            for i in range(2):
                high, low = split16(words(h, r0, i))
                for j, v in ((i, high), (i + 2, low)):
                    ih[dst, 128 * j : 128 * j + 128], il[dst, 128 * j : 128 * j + 128] = two_bf16(v)

    def weigh(lo, size):
        rows = slice(lo, lo + size)
        for s, ref in ((0, amp), (1, phi)):
            cs = coef[s, rows, :]
            ref[rows, :] = lax.dot_general(
                cs, ih[...], NT, preferred_element_type=jnp.float32
            ) + lax.dot_general(cs, il[...], NT, preferred_element_type=jnp.float32)

    copies[0].wait()
    copies[1].wait()
    copies[3].wait()
    weigh(0, first)

    lane = lax.broadcasted_iota(jnp.int32, (32, 128), 1)
    for h in range(2):
        for r0 in range(0, half, 32):
            word = words(h, r0, 2)
            scale = jnp.exp2(-word[:, 127:].astype(jnp.float32)) * (C2 / UP)
            unit_of[h * half + r0 : h * half + r0 + 32, :] = jnp.broadcast_to(scale, (32, 128))
            high, low = split16(word)
            p1 = (high + 64) >> 7
            p2 = high - (p1 << 7)
            p3 = (low + 64) >> 7
            v = jnp.where(lane < w3, p1, jnp.where(lane < 2 * w3, p2, p3))
            parts[h * half + r0 : h * half + r0 + 32, :] = v.astype(jnp.float32).astype(jnp.bfloat16)
    which = (lane[:1] % w3) % q
    r = lax.broadcasted_iota(jnp.int32, (8, 128), 1)
    axis = (r % w3) // q
    unit = jnp.where(r < w3, 2.0**-7, jnp.where(r < 2 * w3, 2.0**-14, 2.0**-22))
    pick = (lax.broadcasted_iota(jnp.int32, (8, 128), 0) == axis) & (r < 3 * w3)
    spread = jnp.where(pick, unit, 0.0).astype(jnp.bfloat16)
    tr = triples[...].astype(jnp.float32).T.astype(jnp.bfloat16)
    bt[...] = jnp.dot(tr, spread, preferred_element_type=jnp.float32).astype(jnp.bfloat16)

    def polar(lo, count):
        total = base[...]
        for g in range(lo, lo + count, 16):
            rows = slice(g, g + 16)
            a, b = amp[rows, :], phi[rows, :]
            h = jnp.maximum(a * a + b * b, 1e-36)
            r = lax.rsqrt(h)
            size = h * r
            x = (b * r) * lax.rsqrt(1.0 + jnp.abs(a) * r)
            x2 = x * x
            ang = (((T[3] * x2 + T[2]) * x2 + T[1]) * x2 + T[0]) * x
            amp[rows, :] = size
            phi[rows, :] = jnp.where(a < 0.0, 0.5 - ang, ang)
            total = total + size[:8] + size[8:]
        base[...] = total

    def angles(k, ref):
        mask = jnp.where(which == k, 1.0, 0.0).astype(jnp.bfloat16)
        ref[...] = lax.dot_general(
            bt[...], parts[...] * mask, NT, preferred_element_type=jnp.float32
        )

    def contract(k, ref):
        acc = jnp.zeros((8, n), jnp.float32)
        for g in range(0, waves, 8):
            rows = slice(g, g + 8)
            v = ref[rows, :] - phi[rows, :]
            v = v - jnp.round(v)
            s = v * v
            w = (s + C1) * s + C0
            acc = acc + (w * w) * amp[rows, :]
        rows_out[pl.ds(k, 1), :] = jnp.sum(acc - base[...], axis=0, keepdims=True)

    copies[2].wait()
    copies[4].wait()
    base[...] = jnp.zeros_like(base)
    lo = 0
    for i, (size, ahead) in enumerate(zip(CHUNKS, CHUNKS[1:])):
        weigh(lo + size, ahead)
        if i == 2:
            angles(0, ua)
        polar(lo, size)
        lo += size
    polar(lo, CHUNKS[-1])
    base[...] = base[...] * MEAN

    for k in range(q):
        held, free = (ua, ub) if k % 2 == 0 else (ub, ua)
        if k + 1 < q:
            angles(k + 1, free)
        contract(k, held)
    for h in range(2):
        turned = rows_out[:, h * half : h * half + half].T
        out[pl.ds(h, half, stride=2), :] = (turned * unit_of[h * half : h * half + half, :])[:, :q]


def partial_ratios(own, mate, coefficients, triples, n, q):
    waves = triples.shape[1]
    orbitals = coefficients.shape[2]
    vmem = pl.BlockSpec(memory_space=pltpu.VMEM)
    hbm = pl.BlockSpec(memory_space=pltpu.HBM)
    return pl.pallas_call(
        wave_kernel,
        out_shape=jax.ShapeDtypeStruct((n, q), jnp.float32),
        in_specs=[vmem, vmem, hbm, hbm],
        out_specs=vmem,
        scratch_shapes=[
            pltpu.VMEM(coefficients.shape, jnp.bfloat16),
            pltpu.VMEM((8, waves), jnp.int32),
            pltpu.VMEM((n, orbitals), jnp.bfloat16),
            pltpu.VMEM((n, orbitals), jnp.bfloat16),
            pltpu.VMEM((n, 128), jnp.bfloat16),
            pltpu.VMEM((waves, 128), jnp.bfloat16),
            pltpu.VMEM((waves, n), jnp.float32),
            pltpu.VMEM((waves, n), jnp.float32),
            pltpu.VMEM((waves, n), jnp.float32),
            pltpu.VMEM((waves, n), jnp.float32),
            pltpu.VMEM((128, n), jnp.float32),
            pltpu.VMEM((8, n), jnp.float32),
            pltpu.VMEM((n, 128), jnp.float32),
            pltpu.SemaphoreType.DMA((5,)),
        ],
        compiler_params=pltpu.CompilerParams(vmem_limit_bytes=52 << 20),
        name="waves",
    )(own, mate, coefficients, triples)


def on_device(
    coefficients, triples, elec_pos, ion_pos, assignment, rotation, quad_table, inverse_rows, n
):
    q = quad_table.shape[2]
    half = n // 2
    msg, kept = pack(
        rotation, assignment, inverse_rows, elec_pos, ion_pos, quad_table, triples, half
    )
    sides = [list(range(c, n, 2)) for c in range(2)]
    own = lax.all_to_all(
        msg.reshape(half, 1, 384), AXES, 0, 0, axis_index_groups=sides, tiled=True
    ).reshape(3 * half, 128)
    mate = lax.ppermute(own, AXES, [(i, i ^ 1) for i in range(n)])
    part = partial_ratios(own, mate, coefficients, kept, n, q)
    back = lax.all_to_all(part.reshape(n, 1, q), AXES, 0, 0, tiled=True)
    return jnp.sum(back, axis=0)


def solution(mesh):
    n = mesh.shape["ga"] * mesh.shape["orb"]
    return jax.shard_map(
        functools.partial(on_device, n=n),
        mesh=mesh,
        in_specs=(
            P(None, AXES, None),
            P(None, AXES),
            P(None, AXES),
            P(),
            P(AXES),
            P(AXES),
            P(),
            P(AXES, None),
        ),
        out_specs=P(AXES, None),
        check_vma=False,
    )
```

```python
import functools

import jax
import jax.numpy as jnp
from jax import lax
from jax.experimental import pallas as pl
from jax.experimental.pallas import tpu as pltpu
from jax.sharding import PartitionSpec as P

AXES = ("ga", "orb")
UP = 2.0**40
KEPT_ROWS = 640
CHUNKS = (128, 256, 256, 256, 256)
C0, C1, C2 = 0.26392367, -1.2978812, 28.72800057
MEAN = 0.0348596450351644
T = tuple(
    t * 2.0 ** (0.5 - i) for i, t in enumerate((0.15911832, 0.02740563, 0.00639816, 0.01881423))
)


def pack_kernel(rot, asg, inv, elec, ion, table, triples, msg, kept, eight, block, sem, sends_sem):
    eight[...] = jnp.zeros_like(eight)
    eight[0:3, :] = triples[...]
    keep = pltpu.make_async_copy(eight, kept.at[pl.ds(0, 8), :], sem)
    keep.start()
    row = inv[...]
    big = jnp.max(jnp.abs(row), axis=1, keepdims=True)
    safe = jnp.maximum(big, 1e-30)
    power = jnp.floor(jnp.log2(32767.0 / safe))
    n16 = jnp.clip(jnp.round(row * jnp.exp2(power)), -32767.0, 32767.0).astype(jnp.int32)
    half = row.shape[1] // 2
    words = n16[:, :half] * 65536 + n16[:, half:]

    lane = lax.broadcasted_iota(jnp.int32, ion.shape, 1)
    home = jnp.sum(jnp.where(lane == asg[0], ion[...], 0.0), axis=1, keepdims=True)
    turn = lax.broadcasted_iota(jnp.int32, table.shape[1:], 1)
    total = 0.0
    homes = []
    for c in range(3):
        h = home[c : c + 1, :]
        off = elec[:, c : c + 1] - h
        homes.append(h)
        total = total + off * off
    radius = jnp.sqrt(total)
    rows = []
    for c in range(3):
        shift = jnp.sum(jnp.where(turn == rot[0], table[c], 0.0), axis=1, keepdims=True)
        x = homes[c] + radius * shift
        x = x - jnp.round(x)
        y = x * 16384.0
        hi = jnp.round(y)
        lo = jnp.round((y - hi) * 32768.0)
        rows.append(hi.astype(jnp.int32) * 65536 + lo.astype(jnp.int32))
    flat = jnp.concatenate(rows, axis=0)
    used = 3 * flat.shape[0]
    column = jnp.concatenate(
        [flat, flat, flat, jnp.zeros((127 - used, 1), jnp.int32), power.astype(jnp.int32)], axis=0
    )
    square = jnp.broadcast_to(column, (128, 128)).T
    coords = square[:24]
    r = lax.broadcasted_iota(jnp.int32, (24, 128), 0) % 3
    tile = jnp.where(
        r == 0,
        jnp.broadcast_to(words[:, :128], (24, 128)),
        jnp.where(r == 1, jnp.broadcast_to(words[:, 128:], (24, 128)), coords),
    )
    block[...] = tile
    sends = [
        pltpu.make_async_copy(block, msg.at[pl.ds(24 * i, 24), :], sends_sem.at[i])
        for i in range(msg.shape[0] // 24)
    ]
    for send in sends:
        send.start()
    for send in sends:
        send.wait()
    keep.wait()


def pack(rotation, assignment, inverse_rows, elec_pos, ion_pos, quad_table, triples, n):
    vmem = pl.BlockSpec(memory_space=pltpu.VMEM)
    smem = pl.BlockSpec(memory_space=pltpu.SMEM)
    return pl.pallas_call(
        pack_kernel,
        in_specs=[smem, smem, vmem, vmem, vmem, vmem, vmem],
        out_specs=[pl.BlockSpec(memory_space=pltpu.HBM)] * 2,
        out_shape=[
            jax.ShapeDtypeStruct((3 * n, 128), jnp.int32),
            jax.ShapeDtypeStruct((KEPT_ROWS, triples.shape[1]), jnp.int32),
        ],
        scratch_shapes=[
            pltpu.VMEM((8, triples.shape[1]), jnp.int32),
            pltpu.VMEM((24, 128), jnp.int32),
            pltpu.SemaphoreType.DMA,
            pltpu.SemaphoreType.DMA((n // 8,)),
        ],
        name="pack",
    )(
        rotation,
        assignment,
        inverse_rows,
        elec_pos.T,
        ion_pos,
        jnp.transpose(quad_table, (1, 2, 0)),
        triples,
    )


def split16(word):
    low = (word << 16) >> 16
    high = (word - low) >> 16
    return high, low


def two_bf16(v):
    f = v.astype(jnp.float32) * UP
    top = f.astype(jnp.bfloat16)
    return top, (f - top.astype(jnp.float32)).astype(jnp.bfloat16)


NT = (((1,), (1,)), ((), ()))
TN = (((0,), (0,)), ((), ()))


def wave_kernel(
    own, mate, coef_hbm, triples_hbm, out, coef, triples, ih, il, parts, bt, amp, phi, ua, ub, rows_out, base, unit_of, sem
):
    n = ih.shape[0]
    half = n // 2
    waves = triples.shape[1]
    q = out.shape[1]
    first = CHUNKS[0]
    copies = [pltpu.make_async_copy(triples_hbm.at[pl.ds(0, 8), :], triples, sem.at[0])]
    for s in range(2):
        for lo, size in ((0, first), (first, waves - first)):
            copies.append(
                pltpu.make_async_copy(
                    coef_hbm.at[s, pl.ds(lo, size), :],
                    coef.at[s, pl.ds(lo, size), :],
                    sem.at[len(copies)],
                )
            )
    for c in (0, 1, 3, 2, 4):
        copies[c].start()
    odd = lax.axis_index("orb") % 2
    w3 = 3 * q

    def words(h, r0, i):
        at = pl.ds(i + 3 * r0, 32, stride=3)
        return jnp.where(odd == h, own[at, :], mate[at, :])

    for h in range(2):
        for r0 in range(0, half, 32):
            dst = slice(h * half + r0, h * half + r0 + 32)
            for i in range(2):
                high, low = split16(words(h, r0, i))
                for j, v in ((i, high), (i + 2, low)):
                    ih[dst, 128 * j : 128 * j + 128], il[dst, 128 * j : 128 * j + 128] = two_bf16(v)

    def weigh(lo, size):
        rows = slice(lo, lo + size)
        for s, ref in ((0, amp), (1, phi)):
            cs = coef[s, rows, :]
            ref[rows, :] = lax.dot_general(
                cs, ih[...], NT, preferred_element_type=jnp.float32
            ) + lax.dot_general(cs, il[...], NT, preferred_element_type=jnp.float32)

    copies[0].wait()
    copies[1].wait()
    copies[3].wait()
    weigh(0, first)

    lane = lax.broadcasted_iota(jnp.int32, (32, 128), 1)
    for h in range(2):
        for r0 in range(0, half, 32):
            word = words(h, r0, 2)
            scale = jnp.exp2(-word[:, 127:].astype(jnp.float32)) * (C2 / UP)
            unit_of[h * half + r0 : h * half + r0 + 32, :] = jnp.broadcast_to(scale, (32, 128))
            high, low = split16(word)
            p1 = (high + 64) >> 7
            p2 = high - (p1 << 7)
            p3 = (low + 64) >> 7
            v = jnp.where(lane < w3, p1, jnp.where(lane < 2 * w3, p2, p3))
            parts[h * half + r0 : h * half + r0 + 32, :] = v.astype(jnp.float32).astype(jnp.bfloat16)
    which = (lane[:1] % w3) % q
    r = lax.broadcasted_iota(jnp.int32, (8, 128), 1)
    axis = (r % w3) // q
    unit = jnp.where(r < w3, 2.0**-7, jnp.where(r < 2 * w3, 2.0**-14, 2.0**-22))
    pick = (lax.broadcasted_iota(jnp.int32, (8, 128), 0) == axis) & (r < 3 * w3)
    spread = jnp.where(pick, unit, 0.0).astype(jnp.bfloat16)
    tr = triples[...].astype(jnp.float32).T.astype(jnp.bfloat16)
    bt[...] = jnp.dot(tr, spread, preferred_element_type=jnp.float32).astype(jnp.bfloat16)

    def polar(lo, count):
        total = base[...]
        for g in range(lo, lo + count, 16):
            rows = slice(g, g + 16)
            a, b = amp[rows, :], phi[rows, :]
            h = jnp.maximum(a * a + b * b, 1e-36)
            r = lax.rsqrt(h)
            size = h * r
            x = (b * r) * lax.rsqrt(1.0 + jnp.abs(a) * r)
            x2 = x * x
            ang = (((T[3] * x2 + T[2]) * x2 + T[1]) * x2 + T[0]) * x
            amp[rows, :] = size
            phi[rows, :] = jnp.where(a < 0.0, 0.5 - ang, ang)
            total = total + size[:8] + size[8:]
        base[...] = total

    def angles(k, ref):
        mask = jnp.where(which == k, 1.0, 0.0).astype(jnp.bfloat16)
        ref[...] = lax.dot_general(
            bt[...], parts[...] * mask, NT, preferred_element_type=jnp.float32
        )

    def contract(k, ref):
        acc = jnp.zeros((8, n), jnp.float32)
        for g in range(0, waves, 8):
            rows = slice(g, g + 8)
            v = ref[rows, :] - phi[rows, :]
            v = v - jnp.round(v)
            s = v * v
            w = (s + C1) * s + C0
            acc = acc + (w * w) * amp[rows, :]
        rows_out[pl.ds(k, 1), :] = jnp.sum(acc - base[...], axis=0, keepdims=True)

    copies[2].wait()
    copies[4].wait()
    base[...] = jnp.zeros_like(base)
    lo = 0
    for i, (size, ahead) in enumerate(zip(CHUNKS, CHUNKS[1:])):
        weigh(lo + size, ahead)
        if i == 2:
            angles(0, ua)
        polar(lo, size)
        lo += size
    polar(lo, CHUNKS[-1])
    base[...] = base[...] * MEAN

    for k in range(q):
        held, free = (ua, ub) if k % 2 == 0 else (ub, ua)
        if k + 1 < q:
            angles(k + 1, free)
        contract(k, held)
    for h in range(2):
        turned = rows_out[:, h * half : h * half + half].T
        out[pl.ds(h, half, stride=2), :] = (turned * unit_of[h * half : h * half + half, :])[:, :q]


def partial_ratios(own, mate, coefficients, triples, n, q):
    waves = triples.shape[1]
    orbitals = coefficients.shape[2]
    vmem = pl.BlockSpec(memory_space=pltpu.VMEM)
    hbm = pl.BlockSpec(memory_space=pltpu.HBM)
    return pl.pallas_call(
        wave_kernel,
        out_shape=jax.ShapeDtypeStruct((n, q), jnp.float32),
        in_specs=[vmem, vmem, hbm, hbm],
        out_specs=vmem,
        scratch_shapes=[
            pltpu.VMEM(coefficients.shape, jnp.bfloat16),
            pltpu.VMEM((8, waves), jnp.int32),
            pltpu.VMEM((n, orbitals), jnp.bfloat16),
            pltpu.VMEM((n, orbitals), jnp.bfloat16),
            pltpu.VMEM((n, 128), jnp.bfloat16),
            pltpu.VMEM((waves, 128), jnp.bfloat16),
            pltpu.VMEM((waves, n), jnp.float32),
            pltpu.VMEM((waves, n), jnp.float32),
            pltpu.VMEM((waves, n), jnp.float32),
            pltpu.VMEM((waves, n), jnp.float32),
            pltpu.VMEM((128, n), jnp.float32),
            pltpu.VMEM((8, n), jnp.float32),
            pltpu.VMEM((n, 128), jnp.float32),
            pltpu.SemaphoreType.DMA((5,)),
        ],
        compiler_params=pltpu.CompilerParams(vmem_limit_bytes=52 << 20),
        name="waves",
    )(own, mate, coefficients, triples)


def on_device(
    coefficients, triples, elec_pos, ion_pos, assignment, rotation, quad_table, inverse_rows, n
):
    q = quad_table.shape[2]
    half = n // 2
    msg, kept = pack(
        rotation, assignment, inverse_rows, elec_pos, ion_pos, quad_table, triples, half
    )
    sides = [list(range(c, n, 2)) for c in range(2)]
    own = lax.all_to_all(
        msg.reshape(half, 1, 384), AXES, 0, 0, axis_index_groups=sides, tiled=True
    ).reshape(3 * half, 128)
    mate = lax.ppermute(own, AXES, [(i, i ^ 1) for i in range(n)])
    part = partial_ratios(own, mate, coefficients, kept, n, q)
    back = lax.all_to_all(part.reshape(n, 1, q), AXES, 0, 0, tiled=True)
    return jnp.sum(back, axis=0)


def solution(mesh):
    n = mesh.shape["ga"] * mesh.shape["orb"]
    return jax.shard_map(
        functools.partial(on_device, n=n),
        mesh=mesh,
        in_specs=(
            P(None, AXES, None),
            P(None, AXES),
            P(None, AXES),
            P(),
            P(AXES),
            P(AXES),
            P(),
            P(AXES, None),
        ),
        out_specs=P(AXES, None),
        check_vma=False,
    )
```
